256 devices in a mesh: dp: 2 (over y_hi), seq: 128 (over y_lo, z, x, core).
Axes of the slice: x: 4, y: 4 (y_hi: 2, y_lo: 2; y = y_hi * 2 + y_lo), z: 8, core: 2. Of those that a mesh axis runs over, the one named last changes fastest.
Arguments:
- values: bfloat16 [2, 32768, 256], P('dp', 'seq'), may hold values from -6 to 6
- gate_acts: bfloat16 [2, 32768, 256], P('dp', 'seq'), may hold values from -6 to 6
- filter_taps: bfloat16 [32768, 256], P('seq'), may hold values from -1.4 to 1.4
- skip_bias: float32 [256], replicated, may hold values from 0.25 to 1.75
- grad_out: bfloat16 [2, 32768, 256], P('dp', 'seq'), may hold values from -6 to 6
Outputs:
- mixed_out: bfloat16 [2, 32768, 256], P('dp', 'seq')
- grad_values: bfloat16 [2, 32768, 256], P('dp', 'seq')
- grad_gates: bfloat16 [2, 32768, 256], P('dp', 'seq')
- grad_filter: float32 [32768, 256], P('seq', 'dp')
The draws below stay inside these ranges and needn't reach their ends.
All inputs are finite; a program needn't handle non-finite values.
Results may differ from the reference program's by a relative error of at most 0.007.
Values may be sent and summed in bfloat16 or wider, within the bound.
A program may use at most 64 MiB of HBM per device.

```python
import math
import jax
import jax.numpy as jnp
from jax import lax

C = 256
L = 32768
BATCH = 2


window_shift = 0.1


def draw_filter_taps(key, part):
    noise_key, rate_key = jax.random.split(jax.random.fold_in(key, 11))
    decay_span = jnp.exp(jax.random.uniform(rate_key, (C,), jnp.float32, math.log(40.0), math.log(4.0 * L)))
    position = jnp.arange(L, dtype=jnp.float32)[:, None]
    envelope = jnp.exp(-position / decay_span[None, :]) + window_shift
    square_sum = jnp.expm1(-2.0 * L / decay_span) / jnp.expm1(-2.0 / decay_span)
    drawn_sum = jnp.expm1(-1.0 * L / decay_span) / jnp.expm1(-1.0 / decay_span)
    energy = square_sum + 2.0 * window_shift * drawn_sum + window_shift * window_shift * L
    amplitude = 1.0 / jnp.sqrt(energy)
    noise = jnp.clip(jax.random.normal(noise_key, (L, C), jnp.float32), -6.0, 6.0)
    return (noise * envelope * amplitude[None, :]).astype(jnp.bfloat16)


def block_scale(own_key, dims, cuts, low, high):
    def one(axis_at, shards_of):
        draws = jax.random.uniform(jax.random.fold_in(jax.random.fold_in(own_key, 6), axis_at), (shards_of,), jnp.float32, low / len(cuts), high / len(cuts))
        return jnp.repeat(jnp.exp(draws), dims[axis_at] // shards_of).reshape((-1,) + (1,) * (len(dims) - axis_at - 1))

    gain = one(*cuts[0])
    for cut in cuts[1:]:
        gain = gain * one(*cut)
    return gain


def gaussian(rng, shape, deviation, most, cuts=(), kind=jnp.bfloat16):
    factor_of = block_scale(rng, shape, cuts, -0.22, 0.18) if cuts else 1.0
    values = jax.random.normal(rng, shape, jnp.float32) * deviation * factor_of
    return jnp.minimum(jnp.maximum(values, -most), most).astype(kind)


def setup_inputs(seed: int = 0) -> dict:
    key_of = jax.random.split(jax.random.key(seed), 6)
    values = gaussian(key_of[0], (BATCH, L, C), 1.0, 6.0, ((0, 2), (1, 128)))
    gate_acts = gaussian(key_of[1], (BATCH, L, C), 1.0, 6.0, ((0, 2), (1, 128)))
    filter_taps = draw_filter_taps(jax.random.fold_in(key_of[5], 71), 0)
    skip_bias = jnp.clip(jax.random.uniform(key_of[3], (C,), jnp.float32, 0.25, 1.75), 0.25, 1.75)
    grad_out = gaussian(key_of[4], (BATCH, L, C), 1.0, 6.0, ((0, 2), (1, 128)))
    return {"values": values, "gate_acts": gate_acts, "filter_taps": filter_taps, "skip_bias": skip_bias, "grad_out": grad_out}


def one_group(values, gate_acts, filter_taps, skip_bias, grad_out):
    length = values.shape[1]
    padded = 2 * length
    signal = values.astype(jnp.float32)
    gate_vals = gate_acts.astype(jnp.float32)
    cotangent = grad_out.astype(jnp.float32)
    spec_values = jnp.fft.rfft(signal, n=padded, axis=1)
    spec_taps = jnp.fft.rfft(filter_taps.astype(jnp.float32), n=padded, axis=0)[None]
    conv_part = jnp.fft.irfft(spec_values * spec_taps, n=padded, axis=1)[:, :length]
    hyena_pre = conv_part + skip_bias * signal
    mixed_out = (gate_vals * hyena_pre).astype(jnp.bfloat16)
    gate_grad = (cotangent * gate_vals).astype(jnp.bfloat16)
    gate_back = lax.optimization_barrier(gate_grad).astype(jnp.float32)
    grad_gates = (cotangent * hyena_pre).astype(jnp.bfloat16)
    spec_grad = jnp.fft.rfft(gate_back, n=padded, axis=1)
    back_part = jnp.fft.irfft(spec_grad * jnp.conj(spec_taps), n=padded, axis=1)[:, :length]
    grad_values = (back_part + skip_bias * gate_back).astype(jnp.bfloat16)
    spec_filter = lax.optimization_barrier(jnp.sum(jnp.conj(spec_values) * spec_grad, axis=0))
    scale_factor = 1.0 / math.sqrt(values.shape[0] * length)
    grad_filter = jnp.fft.irfft(spec_filter, n=padded, axis=0)[:length] * scale_factor
    return (mixed_out, grad_values, grad_gates, grad_filter)

def reference(values, gate_acts, filter_taps, skip_bias, grad_out):
    group_width = math.gcd(C, 32)
    group_count = C // group_width

    def split_batch(array):
        return array.reshape(array.shape[0], array.shape[1], group_count, group_width).transpose(2, 0, 1, 3)

    def join_batch(array):
        return array.transpose(1, 2, 0, 3).reshape(array.shape[1], array.shape[2], C)
    tap_groups = filter_taps.reshape(L, group_count, group_width).transpose(1, 0, 2)
    bias_groups = skip_bias.reshape(group_count, group_width)

    def run_group(operands):
        return one_group(operands[0], operands[1], operands[2], operands[3], operands[4])
    results = lax.map(run_group, (split_batch(values), split_batch(gate_acts), tap_groups, bias_groups, split_batch(grad_out)))
    grad_filter = results[3].transpose(1, 0, 2).reshape(L, C)
    return (join_batch(results[0]), join_batch(results[1]), join_batch(results[2]), grad_filter)
```

```python
import math

import jax
import jax.numpy as jnp
from jax import lax
from jax.sharding import PartitionSpec as P

ALL = ("dp", "seq")

precise = lax.Precision.HIGHEST


def contract(pattern, left, right):
    return jnp.einsum(
        pattern, left, right, precision=precise, preferred_element_type=jnp.float32
    )


def angles(first_idx, second_idx, period):
    turns = first_idx[:, None] * second_idx[None, :] % period
    phase = turns.astype(jnp.float32) * (2.0 * math.pi / period)
    return (jnp.cos(phase), jnp.sin(phase))


def spectra(signal, outer, inner):
    half = outer // 2
    padded = outer * inner
    k_idx = jnp.arange(outer, dtype=jnp.int32)
    a_idx = jnp.arange(half, dtype=jnp.int32)
    b_idx = jnp.arange(inner, dtype=jnp.int32)
    cos1, sin1 = angles(k_idx, a_idx, outer)
    y_re = contract("ka,xab->xkb", cos1, signal)
    y_im = -contract("ka,xab->xkb", sin1, signal)
    tw_re, tw_im = angles(k_idx, b_idx, padded)
    y_re, y_im = (y_re * tw_re + y_im * tw_im, y_im * tw_re - y_re * tw_im)
    cos2, sin2 = angles(b_idx, b_idx, inner)
    z_re = contract("xkb,bl->xkl", y_re, cos2) + contract("xkb,bl->xkl", y_im, sin2)
    z_im = contract("xkb,bl->xkl", y_im, cos2) - contract("xkb,bl->xkl", y_re, sin2)
    return z_re, z_im


def timeline(z_re, z_im, outer, inner):
    half = outer // 2
    padded = outer * inner
    k_idx = jnp.arange(outer, dtype=jnp.int32)
    a_idx = jnp.arange(half, dtype=jnp.int32)
    b_idx = jnp.arange(inner, dtype=jnp.int32)
    cos2, sin2 = angles(b_idx, b_idx, inner)
    u_re = contract("xkl,lb->xkb", z_re, cos2) - contract("xkl,lb->xkb", z_im, sin2)
    u_im = contract("xkl,lb->xkb", z_im, cos2) + contract("xkl,lb->xkb", z_re, sin2)
    tw_re, tw_im = angles(k_idx, b_idx, padded)
    u_re, u_im = (u_re * tw_re - u_im * tw_im, u_im * tw_re + u_re * tw_im)
    cos1, sin1 = angles(a_idx, k_idx, outer)
    signal = contract("ak,xkb->xab", cos1, u_re) - contract("ak,xkb->xab", sin1, u_im)
    return signal * (1.0 / padded)


def on_device(values, gate_acts, filter_taps, skip_bias, grad_out):
    dp_count = lax.axis_size("dp")
    seq_count = lax.axis_size("seq")
    dev_count = dp_count * seq_count
    dp_index = lax.axis_index("dp")
    me = dp_index * seq_count + lax.axis_index("seq")
    rows = values.shape[1]
    channels = values.shape[2]
    per = channels // dev_count
    tap_rows = rows // dp_count

    taps_part = lax.dynamic_slice_in_dim(filter_taps, dp_index * tap_rows, tap_rows, 0)
    send = jnp.concatenate(
        [values[0].T, gate_acts[0].T, grad_out[0].T, taps_part.T], axis=1
    ).reshape(dev_count, per, 3 * rows + tap_rows)
    got = lax.all_to_all(send, ALL, 0, 0, tiled=True)

    def owned(lo, width):
        part = got[:, :, lo : lo + width].reshape(dp_count, seq_count, per, width)
        return part.transpose(2, 0, 1, 3)

    val = owned(0, rows)
    gate = owned(rows, rows)
    cot = owned(2 * rows, rows)
    taps = owned(3 * rows, tap_rows).transpose(0, 2, 1, 3).reshape(per, 1, seq_count, rows)
    grad_sig = (cot.astype(jnp.float32) * gate.astype(jnp.float32)).astype(jnp.bfloat16)

    outer = 2 * seq_count
    signal = jnp.concatenate([val, grad_sig, taps], axis=1).astype(jnp.float32)
    kinds = signal.shape[1]
    z_re, z_im = spectra(signal.reshape(per * kinds, seq_count, rows), outer, rows)
    z_re = z_re.reshape(per, kinds, outer, rows)
    z_im = z_im.reshape(per, kinds, outer, rows)
    v_re, v_im = z_re[:, :dp_count], z_im[:, :dp_count]
    g_re, g_im = z_re[:, dp_count : 2 * dp_count], z_im[:, dp_count : 2 * dp_count]
    t_re, t_im = z_re[:, 2 * dp_count :], z_im[:, 2 * dp_count :]
    conv_re = v_re * t_re - v_im * t_im
    conv_im = v_re * t_im + v_im * t_re
    corr_re = g_re * t_re + g_im * t_im
    corr_im = g_im * t_re - g_re * t_im
    filt_re = jnp.sum(v_re * g_re + v_im * g_im, axis=1, keepdims=True)
    filt_im = jnp.sum(v_re * g_im - v_im * g_re, axis=1, keepdims=True)
    prod_re = jnp.concatenate([conv_re, corr_re, filt_re], axis=1)
    prod_im = jnp.concatenate([conv_im, corr_im, filt_im], axis=1)
    out = timeline(
        prod_re.reshape(per * kinds, outer, rows),
        prod_im.reshape(per * kinds, outer, rows),
        outer,
        rows,
    ).reshape(per, kinds, seq_count, rows)
    conv_part = out[:, :dp_count]
    back_part = out[:, dp_count : 2 * dp_count]
    total = dp_count * seq_count * rows
    grad_filter = out[:, 2 * dp_count] * (1.0 / math.sqrt(total))

    bias = lax.dynamic_slice_in_dim(skip_bias, me * per, per, 0)[:, None, None, None]
    hyena_pre = conv_part + bias * val.astype(jnp.float32)
    mixed_out = (gate.astype(jnp.float32) * hyena_pre).astype(jnp.bfloat16)
    grad_gates = (cot.astype(jnp.float32) * hyena_pre).astype(jnp.bfloat16)
    grad_values = (back_part + bias * grad_sig.astype(jnp.float32)).astype(jnp.bfloat16)

    back = jnp.concatenate([mixed_out, grad_values, grad_gates], axis=3)
    back = back.transpose(1, 2, 0, 3).reshape(dev_count, per, 3 * rows)
    back = lax.all_to_all(back, ALL, 0, 0, tiled=True).reshape(channels, 3, rows)
    mixed_out = back[:, 0].T[None]
    grad_values = back[:, 1].T[None]
    grad_gates = back[:, 2].T[None]

    filt = lax.all_to_all(grad_filter.transpose(1, 0, 2), "seq", 0, 0, tiled=True)
    grad_filter = filt.reshape(seq_count * per, rows).T
    return (mixed_out, grad_values, grad_gates, grad_filter)


def solution(mesh):
    in_specs = (P("dp", "seq", None), P("dp", "seq", None), P("seq", None), P(), P("dp", "seq", None))
    out_specs = (P("dp", "seq", None), P("dp", "seq", None), P("dp", "seq", None), P("seq", "dp"))
    return jax.shard_map(
        on_device, mesh=mesh, in_specs=in_specs, out_specs=out_specs, check_vma=False
    )
```

```python
import math

import jax
import jax.numpy as jnp
from jax import lax
from jax.sharding import PartitionSpec as P

ALL = ("dp", "seq")

precise = lax.Precision.HIGH


def contract(pattern, left, right):
    return jnp.einsum(
        pattern, left, right, precision=precise, preferred_element_type=jnp.float32
    )


def angles(first_idx, second_idx, period):
    turns = first_idx[:, None] * second_idx[None, :] % period
    phase = turns.astype(jnp.float32) * (2.0 * math.pi / period)
    return (jnp.cos(phase), jnp.sin(phase))


def spectra(x_re, x_im, outer, inner):
    half = outer // 2
    padded = outer * inner
    k_idx = jnp.arange(outer, dtype=jnp.int32)
    a_idx = jnp.arange(half, dtype=jnp.int32)
    b_idx = jnp.arange(inner, dtype=jnp.int32)
    cos1, sin1 = angles(k_idx, a_idx, outer)
    y_re = contract("ka,xab->xkb", cos1, x_re) + contract("ka,xab->xkb", sin1, x_im)
    y_im = contract("ka,xab->xkb", cos1, x_im) - contract("ka,xab->xkb", sin1, x_re)
    tw_re, tw_im = angles(k_idx, b_idx, padded)
    y_re, y_im = (y_re * tw_re + y_im * tw_im, y_im * tw_re - y_re * tw_im)
    cos2, sin2 = angles(b_idx, b_idx, inner)
    z_re = contract("xkb,bl->xkl", y_re, cos2) + contract("xkb,bl->xkl", y_im, sin2)
    z_im = contract("xkb,bl->xkl", y_im, cos2) - contract("xkb,bl->xkl", y_re, sin2)
    return z_re, z_im


def timeline(z_re, z_im, outer, inner):
    half = outer // 2
    padded = outer * inner
    k_idx = jnp.arange(outer, dtype=jnp.int32)
    a_idx = jnp.arange(half, dtype=jnp.int32)
    b_idx = jnp.arange(inner, dtype=jnp.int32)
    cos2, sin2 = angles(b_idx, b_idx, inner)
    u_re = contract("xkl,lb->xkb", z_re, cos2) - contract("xkl,lb->xkb", z_im, sin2)
    u_im = contract("xkl,lb->xkb", z_im, cos2) + contract("xkl,lb->xkb", z_re, sin2)
    tw_re, tw_im = angles(k_idx, b_idx, padded)
    u_re, u_im = (u_re * tw_re - u_im * tw_im, u_im * tw_re + u_re * tw_im)
    cos1, sin1 = angles(a_idx, k_idx, outer)
    s_re = contract("ak,xkb->xab", cos1, u_re) - contract("ak,xkb->xab", sin1, u_im)
    s_im = contract("ak,xkb->xab", cos1, u_im) + contract("ak,xkb->xab", sin1, u_re)
    return s_re * (1.0 / padded), s_im * (1.0 / padded)


def on_device(values, gate_acts, filter_taps, skip_bias, grad_out):
    dp_count = lax.axis_size("dp")
    seq_count = lax.axis_size("seq")
    dev_count = dp_count * seq_count
    dp_index = lax.axis_index("dp")
    me = dp_index * seq_count + lax.axis_index("seq")
    rows = values.shape[1]
    channels = values.shape[2]
    per = channels // dev_count
    tap_rows = rows // dp_count

    taps_part = lax.dynamic_slice_in_dim(filter_taps, dp_index * tap_rows, tap_rows, 0)
    send = jnp.concatenate(
        [values[0].T, gate_acts[0].T, grad_out[0].T, taps_part.T], axis=1
    ).reshape(dev_count, per, 3 * rows + tap_rows)
    got = lax.all_to_all(send, ALL, 0, 0, tiled=True)

    def owned(lo, width):
        part = got[:, :, lo : lo + width].reshape(dp_count, seq_count, per, width)
        return part.transpose(2, 0, 1, 3)

    val = owned(0, rows)
    gate = owned(rows, rows)
    cot = owned(2 * rows, rows)
    taps = owned(3 * rows, tap_rows).transpose(0, 2, 1, 3).reshape(per, 1, seq_count, rows)
    grad_sig = (cot.astype(jnp.float32) * gate.astype(jnp.float32)).astype(jnp.bfloat16)

    outer = 2 * seq_count
    sig_re = jnp.stack([val[:, 0], grad_sig[:, 0], taps[:, 0]], axis=1).astype(jnp.float32)
    sig_im = jnp.stack(
        [val[:, 1], grad_sig[:, 1], jnp.zeros_like(taps[:, 0])], axis=1
    ).astype(jnp.float32)
    z_re, z_im = spectra(
        sig_re.reshape(per * 3, seq_count, rows), sig_im.reshape(per * 3, seq_count, rows), outer, rows
    )
    z_re = z_re.reshape(per, 3, outer, rows)
    z_im = z_im.reshape(per, 3, outer, rows)
    v_re, v_im = z_re[:, 0], z_im[:, 0]
    g_re, g_im = z_re[:, 1], z_im[:, 1]
    t_re, t_im = z_re[:, 2], z_im[:, 2]
    conv_re = v_re * t_re - v_im * t_im
    conv_im = v_re * t_im + v_im * t_re
    corr_re = g_re * t_re + g_im * t_im
    corr_im = g_im * t_re - g_re * t_im
    filt_re = v_re * g_re + v_im * g_im
    filt_im = v_re * g_im - v_im * g_re
    prod_re = jnp.stack([conv_re, corr_re, filt_re], axis=1).reshape(per * 3, outer, rows)
    prod_im = jnp.stack([conv_im, corr_im, filt_im], axis=1).reshape(per * 3, outer, rows)
    out_re, out_im = timeline(prod_re, prod_im, outer, rows)
    out_re = out_re.reshape(per, 3, seq_count, rows)
    out_im = out_im.reshape(per, 3, seq_count, rows)
    conv_part = jnp.stack([out_re[:, 0], out_im[:, 0]], axis=1)
    back_part = jnp.stack([out_re[:, 1], out_im[:, 1]], axis=1)
    total = dp_count * seq_count * rows
    grad_filter = out_re[:, 2] * (1.0 / math.sqrt(total))

    bias = lax.dynamic_slice_in_dim(skip_bias, me * per, per, 0)[:, None, None, None]
    hyena_pre = conv_part + bias * val.astype(jnp.float32)
    mixed_out = (gate.astype(jnp.float32) * hyena_pre).astype(jnp.bfloat16)
    grad_gates = (cot.astype(jnp.float32) * hyena_pre).astype(jnp.bfloat16)
    grad_values = (back_part + bias * grad_sig.astype(jnp.float32)).astype(jnp.bfloat16)

    back = jnp.concatenate([mixed_out, grad_values, grad_gates], axis=3)
    back = back.transpose(1, 2, 0, 3).reshape(dev_count, per, 3 * rows)
    back = lax.all_to_all(back, ALL, 0, 0, tiled=True).reshape(channels, 3, rows)
    mixed_out = back[:, 0].T[None]
    grad_values = back[:, 1].T[None]
    grad_gates = back[:, 2].T[None]

    filt = lax.all_to_all(grad_filter.transpose(1, 0, 2), "seq", 0, 0, tiled=True)
    grad_filter = filt.reshape(seq_count * per, rows).T
    return (mixed_out, grad_values, grad_gates, grad_filter)


def solution(mesh):
    in_specs = (P("dp", "seq", None), P("dp", "seq", None), P("seq", None), P(), P("dp", "seq", None))
    out_specs = (P("dp", "seq", None), P("dp", "seq", None), P("dp", "seq", None), P("seq", "dp"))
    return jax.shard_map(
        on_device, mesh=mesh, in_specs=in_specs, out_specs=out_specs, check_vma=False
    )
```

```python
import math

import jax
import jax.numpy as jnp
from jax import lax
from jax.sharding import PartitionSpec as P

ALL = ("dp", "seq")

precise = lax.Precision.HIGH


def contract(pattern, left, right):
    return jnp.einsum(
        pattern, left, right, precision=precise, preferred_element_type=jnp.float32
    )


def angles(first_idx, second_idx, period):
    turns = first_idx[:, None] * second_idx[None, :] % period
    phase = turns.astype(jnp.float32) * (2.0 * math.pi / period)
    return (jnp.cos(phase), jnp.sin(phase))


def spectra(x_re, x_im, outer, inner):
    half = outer // 2
    padded = outer * inner
    k_idx = jnp.arange(outer, dtype=jnp.int32)
    a_idx = jnp.arange(half, dtype=jnp.int32)
    b_idx = jnp.arange(inner, dtype=jnp.int32)
    cos1, sin1 = angles(k_idx, a_idx, outer)
    y_re = contract("ka,xab->xkb", cos1, x_re) + contract("ka,xab->xkb", sin1, x_im)
    y_im = contract("ka,xab->xkb", cos1, x_im) - contract("ka,xab->xkb", sin1, x_re)
    tw_re, tw_im = angles(k_idx, b_idx, padded)
    y_re, y_im = (y_re * tw_re + y_im * tw_im, y_im * tw_re - y_re * tw_im)
    cos2, sin2 = angles(b_idx, b_idx, inner)
    z_re = contract("xkb,bl->xkl", y_re, cos2) + contract("xkb,bl->xkl", y_im, sin2)
    z_im = contract("xkb,bl->xkl", y_im, cos2) - contract("xkb,bl->xkl", y_re, sin2)
    return z_re, z_im


def timeline(z_re, z_im, outer, inner):
    half = outer // 2
    padded = outer * inner
    k_idx = jnp.arange(outer, dtype=jnp.int32)
    a_idx = jnp.arange(half, dtype=jnp.int32)
    b_idx = jnp.arange(inner, dtype=jnp.int32)
    cos2, sin2 = angles(b_idx, b_idx, inner)
    u_re = contract("xkl,lb->xkb", z_re, cos2) - contract("xkl,lb->xkb", z_im, sin2)
    u_im = contract("xkl,lb->xkb", z_im, cos2) + contract("xkl,lb->xkb", z_re, sin2)
    tw_re, tw_im = angles(k_idx, b_idx, padded)
    u_re, u_im = (u_re * tw_re - u_im * tw_im, u_im * tw_re + u_re * tw_im)
    cos1, sin1 = angles(a_idx, k_idx, outer)
    s_re = contract("ak,xkb->xab", cos1, u_re) - contract("ak,xkb->xab", sin1, u_im)
    s_im = contract("ak,xkb->xab", cos1, u_im) + contract("ak,xkb->xab", sin1, u_re)
    return s_re * (1.0 / padded), s_im * (1.0 / padded)


def on_device(values, gate_acts, filter_taps, skip_bias, grad_out):
    dp_count = lax.axis_size("dp")
    seq_count = lax.axis_size("seq")
    dev_count = dp_count * seq_count
    dp_index = lax.axis_index("dp")
    me = dp_index * seq_count + lax.axis_index("seq")
    rows = values.shape[1]
    channels = values.shape[2]
    per = channels // dev_count
    tap_rows = rows // dp_count

    taps_part = lax.dynamic_slice_in_dim(filter_taps, dp_index * tap_rows, tap_rows, 0)
    gate_grad = (grad_out[0].astype(jnp.float32) * gate_acts[0].astype(jnp.float32)).astype(
        jnp.bfloat16
    )
    send = jnp.concatenate([values[0].T, gate_grad.T, taps_part.T], axis=1).reshape(
        dev_count, per, 2 * rows + tap_rows
    )
    got = lax.all_to_all(send, ALL, 0, 0, tiled=True)

    def owned(lo, width):
        part = got[:, :, lo : lo + width].reshape(dp_count, seq_count, per, width)
        return part.transpose(2, 0, 1, 3)

    val = owned(0, rows)
    grad_sig = owned(rows, rows)
    taps = owned(2 * rows, tap_rows).transpose(0, 2, 1, 3).reshape(per, 1, seq_count, rows)

    outer = 2 * seq_count
    sig_re = jnp.stack([val[:, 0], grad_sig[:, 0], taps[:, 0]], axis=1).astype(jnp.float32)
    sig_im = jnp.stack(
        [val[:, 1], grad_sig[:, 1], jnp.zeros_like(taps[:, 0])], axis=1
    ).astype(jnp.float32)
    z_re, z_im = spectra(
        sig_re.reshape(per * 3, seq_count, rows), sig_im.reshape(per * 3, seq_count, rows), outer, rows
    )
    z_re = z_re.reshape(per, 3, outer, rows)
    z_im = z_im.reshape(per, 3, outer, rows)
    v_re, v_im = z_re[:, 0], z_im[:, 0]
    g_re, g_im = z_re[:, 1], z_im[:, 1]
    t_re, t_im = z_re[:, 2], z_im[:, 2]
    conv_re = v_re * t_re - v_im * t_im
    conv_im = v_re * t_im + v_im * t_re
    corr_re = g_re * t_re + g_im * t_im
    corr_im = g_im * t_re - g_re * t_im
    filt_re = v_re * g_re + v_im * g_im
    filt_im = v_re * g_im - v_im * g_re
    prod_re = jnp.stack([conv_re, corr_re, filt_re], axis=1).reshape(per * 3, outer, rows)
    prod_im = jnp.stack([conv_im, corr_im, filt_im], axis=1).reshape(per * 3, outer, rows)
    out_re, out_im = timeline(prod_re, prod_im, outer, rows)
    out_re = out_re.reshape(per, 3, seq_count, rows)
    out_im = out_im.reshape(per, 3, seq_count, rows)
    conv_part = jnp.stack([out_re[:, 0], out_im[:, 0]], axis=1)
    back_part = jnp.stack([out_re[:, 1], out_im[:, 1]], axis=1)
    total = dp_count * seq_count * rows
    grad_filter = (out_re[:, 2] * (1.0 / math.sqrt(total))).astype(jnp.bfloat16)

    bias = lax.dynamic_slice_in_dim(skip_bias, me * per, per, 0)[:, None, None, None]
    hyena_pre = (conv_part + bias * val.astype(jnp.float32)).astype(jnp.bfloat16)
    grad_values = (back_part + bias * grad_sig.astype(jnp.float32)).astype(jnp.bfloat16)

    filt_rep = jnp.broadcast_to(grad_filter[:, None], (per, dp_count, seq_count, rows))
    back = jnp.concatenate([hyena_pre, grad_values, filt_rep], axis=3)
    back = back.transpose(1, 2, 0, 3).reshape(dev_count, per, 3 * rows)
    back = lax.all_to_all(back, ALL, 0, 0, tiled=True).reshape(channels, 3, rows)
    hyena_pre = back[:, 0].T.astype(jnp.float32)
    grad_values = back[:, 1].T[None]
    share = channels // dp_count
    grad_filter = lax.dynamic_slice_in_dim(back[:, 2], dp_index * share, share, 0)
    grad_filter = grad_filter.T.astype(jnp.float32)
    mixed_out = (gate_acts[0].astype(jnp.float32) * hyena_pre).astype(jnp.bfloat16)[None]
    grad_gates = (grad_out[0].astype(jnp.float32) * hyena_pre).astype(jnp.bfloat16)[None]
    return (mixed_out, grad_values, grad_gates, grad_filter)


def solution(mesh):
    in_specs = (P("dp", "seq", None), P("dp", "seq", None), P("seq", None), P(), P("dp", "seq", None))
    out_specs = (P("dp", "seq", None), P("dp", "seq", None), P("dp", "seq", None), P("seq", "dp"))
    return jax.shard_map(
        on_device, mesh=mesh, in_specs=in_specs, out_specs=out_specs, check_vma=False
    )
```

```python
import math

import jax
import jax.numpy as jnp
from jax import lax
from jax.sharding import PartitionSpec as P

ALL = ("dp", "seq")

precise = lax.Precision.HIGH


def contract(pattern, left, right):
    return jnp.einsum(
        pattern, left, right, precision=precise, preferred_element_type=jnp.float32
    )


def angles(first_idx, second_idx, period):
    turns = first_idx[:, None] * second_idx[None, :] % period
    phase = turns.astype(jnp.float32) * (2.0 * math.pi / period)
    return (jnp.cos(phase), jnp.sin(phase))


def dft_tables(outer, inner):
    half = outer // 2
    padded = outer * inner
    k_idx = jnp.arange(outer, dtype=jnp.int32)
    a_idx = jnp.arange(half, dtype=jnp.int32)
    b_idx = jnp.arange(inner, dtype=jnp.int32)
    cos1, sin1 = angles(k_idx, a_idx, outer)
    first = jnp.stack(
        [jnp.stack([cos1, sin1], axis=1), jnp.stack([-sin1, cos1], axis=1)], axis=1
    )
    cos2, sin2 = angles(b_idx, b_idx, inner)
    second = jnp.stack(
        [jnp.stack([cos2, -sin2], axis=1), jnp.stack([sin2, cos2], axis=1)], axis=0
    )
    twist = angles(k_idx, b_idx, padded)
    return first, second, twist


def spectra(signal, tables):
    first, second, (tw_re, tw_im) = tables
    y = contract("ksra,xrab->xksb", first, signal)
    y_re, y_im = y[:, :, 0], y[:, :, 1]
    y = jnp.stack([y_re * tw_re + y_im * tw_im, y_im * tw_re - y_re * tw_im], axis=2)
    return contract("xksb,sbtl->xktl", y, second)


def timeline(spec, tables):
    first, second, (tw_re, tw_im) = tables
    padded = spec.shape[1] * spec.shape[3]
    u = contract("xktl,ubtl->xkub", spec, second)
    u_re, u_im = u[:, :, 0], u[:, :, 1]
    u = jnp.stack([u_re * tw_re - u_im * tw_im, u_im * tw_re + u_re * tw_im], axis=2)
    return contract("kuva,xkub->xvab", first, u) * (1.0 / padded)


def on_device(values, gate_acts, filter_taps, skip_bias, grad_out):
    dp_count = lax.axis_size("dp")
    seq_count = lax.axis_size("seq")
    dev_count = dp_count * seq_count
    dp_index = lax.axis_index("dp")
    me = dp_index * seq_count + lax.axis_index("seq")
    rows = values.shape[1]
    channels = values.shape[2]
    per = channels // dev_count
    tap_rows = rows // dp_count

    taps_part = lax.dynamic_slice_in_dim(filter_taps, dp_index * tap_rows, tap_rows, 0)
    gate_grad = (grad_out[0].astype(jnp.float32) * gate_acts[0].astype(jnp.float32)).astype(
        jnp.bfloat16
    )
    send = jnp.concatenate([values[0].T, gate_grad.T, taps_part.T], axis=1).reshape(
        dev_count, per, 2 * rows + tap_rows
    )
    got = lax.all_to_all(send, ALL, 0, 0, tiled=True)

    def owned(lo, width):
        part = got[:, :, lo : lo + width].reshape(dp_count, seq_count, per, width)
        return part.transpose(2, 0, 1, 3)

    val = owned(0, rows)
    grad_sig = owned(rows, rows)
    taps = owned(2 * rows, tap_rows).transpose(0, 2, 1, 3).reshape(per, 1, seq_count, rows)

    outer = 2 * seq_count
    tables = dft_tables(outer, rows)
    signal = jnp.stack(
        [
            val,
            grad_sig,
            jnp.concatenate([taps, jnp.zeros_like(taps)], axis=1),
        ],
        axis=1,
    ).astype(jnp.float32)
    spec = spectra(signal.reshape(per * 3, 2, seq_count, rows), tables)
    spec = spec.reshape(per, 3, outer, 2, rows)
    v_re, v_im = spec[:, 0, :, 0], spec[:, 0, :, 1]
    g_re, g_im = spec[:, 1, :, 0], spec[:, 1, :, 1]
    t_re, t_im = spec[:, 2, :, 0], spec[:, 2, :, 1]
    conv = jnp.stack([v_re * t_re - v_im * t_im, v_re * t_im + v_im * t_re], axis=2)
    corr = jnp.stack([g_re * t_re + g_im * t_im, g_im * t_re - g_re * t_im], axis=2)
    filt = jnp.stack([v_re * g_re + v_im * g_im, v_re * g_im - v_im * g_re], axis=2)
    prod = jnp.stack([conv, corr, filt], axis=1).reshape(per * 3, outer, 2, rows)
    out = timeline(prod, tables).reshape(per, 3, 2, seq_count, rows)
    conv_part = out[:, 0]
    back_part = out[:, 1]
    out_re = out[:, :, 0]
    total = dp_count * seq_count * rows
    grad_filter = (out_re[:, 2] * (1.0 / math.sqrt(total))).astype(jnp.bfloat16)

    bias = lax.dynamic_slice_in_dim(skip_bias, me * per, per, 0)[:, None, None, None]
    hyena_pre = (conv_part + bias * val.astype(jnp.float32)).astype(jnp.bfloat16)
    grad_values = (back_part + bias * grad_sig.astype(jnp.float32)).astype(jnp.bfloat16)

    filt_rep = jnp.broadcast_to(grad_filter[:, None], (per, dp_count, seq_count, rows))
    back = jnp.concatenate([hyena_pre, grad_values, filt_rep], axis=3)
    back = back.transpose(1, 2, 0, 3).reshape(dev_count, per, 3 * rows)
    back = lax.all_to_all(back, ALL, 0, 0, tiled=True).reshape(channels, 3, rows)
    hyena_pre = back[:, 0].T.astype(jnp.float32)
    grad_values = back[:, 1].T[None]
    share = channels // dp_count
    grad_filter = lax.dynamic_slice_in_dim(back[:, 2], dp_index * share, share, 0)
    grad_filter = grad_filter.T.astype(jnp.float32)
    mixed_out = (gate_acts[0].astype(jnp.float32) * hyena_pre).astype(jnp.bfloat16)[None]
    grad_gates = (grad_out[0].astype(jnp.float32) * hyena_pre).astype(jnp.bfloat16)[None]
    return (mixed_out, grad_values, grad_gates, grad_filter)


def solution(mesh):
    in_specs = (P("dp", "seq", None), P("dp", "seq", None), P("seq", None), P(), P("dp", "seq", None))
    out_specs = (P("dp", "seq", None), P("dp", "seq", None), P("dp", "seq", None), P("seq", "dp"))
    return jax.shard_map(
        on_device, mesh=mesh, in_specs=in_specs, out_specs=out_specs, check_vma=False
    )
```

```python
import math

import jax
import jax.numpy as jnp
from jax import lax
from jax.sharding import PartitionSpec as P

ALL = ("dp", "seq")

precise = lax.Precision.HIGH


def contract(pattern, left, right):
    return jnp.einsum(
        pattern, left, right, precision=precise, preferred_element_type=jnp.float32
    )


def angles(first_idx, second_idx, period):
    turns = first_idx[:, None] * second_idx[None, :] % period
    phase = turns.astype(jnp.float32) * (2.0 * math.pi / period)
    return (jnp.cos(phase), jnp.sin(phase))


def dft_tables(outer, inner):
    half = outer // 2
    padded = outer * inner
    k_idx = jnp.arange(outer, dtype=jnp.int32)
    a_idx = jnp.arange(half, dtype=jnp.int32)
    b_idx = jnp.arange(inner, dtype=jnp.int32)
    cos1, sin1 = angles(k_idx, a_idx, outer)
    first = jnp.stack(
        [jnp.stack([cos1, sin1], axis=1), jnp.stack([-sin1, cos1], axis=1)], axis=1
    )
    cos2, sin2 = angles(b_idx, b_idx, inner)
    second = jnp.stack(
        [jnp.stack([cos2, -sin2], axis=1), jnp.stack([sin2, cos2], axis=1)], axis=0
    )
    twist = angles(k_idx, b_idx, padded)
    return first, second, twist


def spectra(signal, tables):
    first, second, (tw_re, tw_im) = tables
    y = contract("ksra,xrab->xksb", first, signal)
    y_re, y_im = y[:, :, 0], y[:, :, 1]
    y = jnp.stack([y_re * tw_re + y_im * tw_im, y_im * tw_re - y_re * tw_im], axis=2)
    return contract("xksb,sbtl->xktl", y, second)


def timeline(spec, tables):
    first, second, (tw_re, tw_im) = tables
    padded = spec.shape[1] * spec.shape[3]
    u = contract("xktl,ubtl->xkub", spec, second)
    u_re, u_im = u[:, :, 0], u[:, :, 1]
    u = jnp.stack([u_re * tw_re - u_im * tw_im, u_im * tw_re + u_re * tw_im], axis=2)
    return contract("kuva,xkub->xvab", first, u) * (1.0 / padded)


def on_device(values, gate_acts, filter_taps, skip_bias, grad_out):
    dp_count = lax.axis_size("dp")
    seq_count = lax.axis_size("seq")
    dev_count = dp_count * seq_count
    dp_index = lax.axis_index("dp")
    me = dp_index * seq_count + lax.axis_index("seq")
    rows = values.shape[1]
    channels = values.shape[2]
    per = channels // dev_count
    tap_rows = rows // dp_count

    taps_part = lax.dynamic_slice_in_dim(filter_taps, dp_index * tap_rows, tap_rows, 0)
    gate_grad = (grad_out[0].astype(jnp.float32) * gate_acts[0].astype(jnp.float32)).astype(
        jnp.bfloat16
    )
    width = 2 * rows + tap_rows
    send = jnp.concatenate([values[0], gate_grad, taps_part], axis=0).T
    send = send.reshape(dev_count, 2, per * width // 2)
    got = lax.all_to_all(send, ALL, 0, 0, tiled=True).reshape(dev_count, per, width)

    def owned(lo, width):
        part = got[:, :, lo : lo + width].reshape(dp_count, seq_count, per, width)
        return part.transpose(2, 0, 1, 3)

    val = owned(0, rows)
    grad_sig = owned(rows, rows)
    taps = owned(2 * rows, tap_rows).transpose(0, 2, 1, 3).reshape(per, 1, seq_count, rows)

    outer = 2 * seq_count
    tables = dft_tables(outer, rows)
    signal = jnp.stack(
        [
            val,
            grad_sig,
            jnp.concatenate([taps, jnp.zeros_like(taps)], axis=1),
        ],
        axis=1,
    ).astype(jnp.float32)
    spec = spectra(signal.reshape(per * 3, 2, seq_count, rows), tables)
    spec = spec.reshape(per, 3, outer, 2, rows)
    v_re, v_im = spec[:, 0, :, 0], spec[:, 0, :, 1]
    g_re, g_im = spec[:, 1, :, 0], spec[:, 1, :, 1]
    t_re, t_im = spec[:, 2, :, 0], spec[:, 2, :, 1]
    conv = jnp.stack([v_re * t_re - v_im * t_im, v_re * t_im + v_im * t_re], axis=2)
    corr = jnp.stack([g_re * t_re + g_im * t_im, g_im * t_re - g_re * t_im], axis=2)
    filt = jnp.stack([v_re * g_re + v_im * g_im, v_re * g_im - v_im * g_re], axis=2)
    prod = jnp.stack([conv, corr, filt], axis=1).reshape(per * 3, outer, 2, rows)
    out = timeline(prod, tables).reshape(per, 3, 2, seq_count, rows)
    conv_part = out[:, 0]
    back_part = out[:, 1]
    out_re = out[:, :, 0]
    total = dp_count * seq_count * rows
    grad_filter = (out_re[:, 2] * (1.0 / math.sqrt(total))).astype(jnp.bfloat16)

    bias = lax.dynamic_slice_in_dim(skip_bias, me * per, per, 0)[:, None, None, None]
    hyena_pre = (conv_part + bias * val.astype(jnp.float32)).astype(jnp.bfloat16)
    grad_values = (back_part + bias * grad_sig.astype(jnp.float32)).astype(jnp.bfloat16)

    filt_rep = jnp.broadcast_to(grad_filter[:, None], (per, dp_count, seq_count, rows))
    back = jnp.concatenate([hyena_pre, grad_values, filt_rep], axis=3)
    back = back.transpose(1, 2, 0, 3).reshape(dev_count, 2, per * 3 * rows // 2)
    back = lax.all_to_all(back, ALL, 0, 0, tiled=True).reshape(channels, 3, rows)
    hyena_pre = back[:, 0].T.astype(jnp.float32)
    grad_values = back[:, 1].T[None]
    share = channels // dp_count
    grad_filter = lax.dynamic_slice_in_dim(back[:, 2], dp_index * share, share, 0)
    grad_filter = grad_filter.T.astype(jnp.float32)
    mixed_out = (gate_acts[0].astype(jnp.float32) * hyena_pre).astype(jnp.bfloat16)[None]
    grad_gates = (grad_out[0].astype(jnp.float32) * hyena_pre).astype(jnp.bfloat16)[None]
    return (mixed_out, grad_values, grad_gates, grad_filter)


def solution(mesh):
    in_specs = (P("dp", "seq", None), P("dp", "seq", None), P("seq", None), P(), P("dp", "seq", None))
    out_specs = (P("dp", "seq", None), P("dp", "seq", None), P("dp", "seq", None), P("seq", "dp"))
    return jax.shard_map(
        on_device, mesh=mesh, in_specs=in_specs, out_specs=out_specs, check_vma=False
    )
```

```python
import math

import jax
import jax.numpy as jnp
from jax import lax
from jax.sharding import PartitionSpec as P

ALL = ("dp", "seq")

precise = lax.Precision.HIGH


def contract(pattern, left, right):
    return jnp.einsum(
        pattern, left, right, precision=precise, preferred_element_type=jnp.float32
    )


def angles(first_idx, second_idx, period):
    turns = first_idx[:, None] * second_idx[None, :] % period
    phase = turns.astype(jnp.float32) * (2.0 * math.pi / period)
    return (jnp.cos(phase), jnp.sin(phase))


def dft_tables(outer, inner):
    half = outer // 2
    padded = outer * inner
    k_idx = jnp.arange(outer, dtype=jnp.int32)
    a_idx = jnp.arange(half, dtype=jnp.int32)
    b_idx = jnp.arange(inner, dtype=jnp.int32)
    cos1, sin1 = angles(k_idx, a_idx, outer)
    first = jnp.stack(
        [jnp.stack([cos1, sin1], axis=1), jnp.stack([-sin1, cos1], axis=1)], axis=1
    )
    cos2, sin2 = angles(b_idx, b_idx, inner)
    second = jnp.stack(
        [jnp.stack([cos2, -sin2], axis=1), jnp.stack([sin2, cos2], axis=1)], axis=0
    )
    twist = angles(k_idx, b_idx, padded)
    return first, second, twist


def spectra(signal, tables):
    first, second, (tw_re, tw_im) = tables
    y = contract("ksra,xrab->xksb", first, signal)
    y_re, y_im = y[:, :, 0], y[:, :, 1]
    y = jnp.stack([y_re * tw_re + y_im * tw_im, y_im * tw_re - y_re * tw_im], axis=2)
    return contract("xksb,sbtl->xktl", y, second)


def timeline(spec, tables):
    first, second, (tw_re, tw_im) = tables
    padded = spec.shape[1] * spec.shape[3]
    u = contract("xktl,ubtl->xkub", spec, second)
    u_re, u_im = u[:, :, 0], u[:, :, 1]
    u = jnp.stack([u_re * tw_re - u_im * tw_im, u_im * tw_re + u_re * tw_im], axis=2)
    return contract("kuva,xkub->xvab", first, u) * (1.0 / padded)


def on_device(values, gate_acts, filter_taps, skip_bias, grad_out):
    dp_count = lax.axis_size("dp")
    seq_count = lax.axis_size("seq")
    dev_count = dp_count * seq_count
    dp_index = lax.axis_index("dp")
    me = dp_index * seq_count + lax.axis_index("seq")
    rows = values.shape[1]
    channels = values.shape[2]
    per = channels // dev_count
    tap_rows = rows // dp_count

    taps_part = lax.dynamic_slice_in_dim(filter_taps, dp_index * tap_rows, tap_rows, 0)
    gate_grad = (grad_out[0].astype(jnp.float32) * gate_acts[0].astype(jnp.float32)).astype(
        jnp.bfloat16
    )
    width = 2 * rows + tap_rows
    spare = (-per * width) % 256
    pad = jnp.zeros((spare // per, channels), values.dtype)
    send = jnp.concatenate([values[0], gate_grad, taps_part, pad], axis=0).T
    send = send.reshape(dev_count, 2, (per * width + spare) // 2)
    got = lax.all_to_all(send, ALL, 0, 0, tiled=True).reshape(dev_count, per, -1)

    def owned(lo, width):
        part = got[:, :, lo : lo + width].reshape(dp_count, seq_count, per, width)
        return part.transpose(2, 0, 1, 3)

    val = owned(0, rows)
    grad_sig = owned(rows, rows)
    taps = owned(2 * rows, tap_rows).transpose(0, 2, 1, 3).reshape(per, 1, seq_count, rows)

    outer = 2 * seq_count
    tables = dft_tables(outer, rows)
    signal = jnp.stack(
        [
            val,
            grad_sig,
            jnp.concatenate([taps, jnp.zeros_like(taps)], axis=1),
        ],
        axis=1,
    ).astype(jnp.float32)
    spec = spectra(signal.reshape(per * 3, 2, seq_count, rows), tables)
    spec = spec.reshape(per, 3, outer, 2, rows)
    v_re, v_im = spec[:, 0, :, 0], spec[:, 0, :, 1]
    g_re, g_im = spec[:, 1, :, 0], spec[:, 1, :, 1]
    t_re, t_im = spec[:, 2, :, 0], spec[:, 2, :, 1]
    conv = jnp.stack([v_re * t_re - v_im * t_im, v_re * t_im + v_im * t_re], axis=2)
    corr = jnp.stack([g_re * t_re + g_im * t_im, g_im * t_re - g_re * t_im], axis=2)
    filt = jnp.stack([v_re * g_re + v_im * g_im, v_re * g_im - v_im * g_re], axis=2)
    prod = jnp.stack([conv, corr, filt], axis=1).reshape(per * 3, outer, 2, rows)
    out = timeline(prod, tables).reshape(per, 3, 2, seq_count, rows)
    conv_part = out[:, 0]
    back_part = out[:, 1]
    out_re = out[:, :, 0]
    total = dp_count * seq_count * rows
    grad_filter = (out_re[:, 2] * (1.0 / math.sqrt(total))).astype(jnp.bfloat16)

    bias = lax.dynamic_slice_in_dim(skip_bias, me * per, per, 0)[:, None, None, None]
    hyena_pre = (conv_part + bias * val.astype(jnp.float32)).astype(jnp.bfloat16)
    grad_values = (back_part + bias * grad_sig.astype(jnp.float32)).astype(jnp.bfloat16)

    filt_rep = jnp.broadcast_to(grad_filter[:, None], (per, dp_count, seq_count, rows))
    back = jnp.concatenate([hyena_pre, grad_values, filt_rep], axis=3)
    back = back.transpose(1, 2, 0, 3).reshape(dev_count, 2, per * 3 * rows // 2)
    back = lax.all_to_all(back, ALL, 0, 0, tiled=True).reshape(channels, 3, rows)
    hyena_pre = back[:, 0].T.astype(jnp.float32)
    grad_values = back[:, 1].T[None]
    share = channels // dp_count
    grad_filter = lax.dynamic_slice_in_dim(back[:, 2], dp_index * share, share, 0)
    grad_filter = grad_filter.T.astype(jnp.float32)
    mixed_out = (gate_acts[0].astype(jnp.float32) * hyena_pre).astype(jnp.bfloat16)[None]
    grad_gates = (grad_out[0].astype(jnp.float32) * hyena_pre).astype(jnp.bfloat16)[None]
    return (mixed_out, grad_values, grad_gates, grad_filter)


def solution(mesh):
    in_specs = (P("dp", "seq", None), P("dp", "seq", None), P("seq", None), P(), P("dp", "seq", None))
    out_specs = (P("dp", "seq", None), P("dp", "seq", None), P("dp", "seq", None), P("seq", "dp"))
    return jax.shard_map(
        on_device, mesh=mesh, in_specs=in_specs, out_specs=out_specs, check_vma=False
    )
```
